512 devices in a mesh: grp: 16 (over y, z_hi), sp: 32 (over z_lo, x, core).
Axes of the slice: x: 4, y: 4, z: 16 (z_hi: 4, z_lo: 4; z = z_hi * 4 + z_lo), core: 2. Of those that a mesh axis runs over, the one named last changes fastest.
Arguments:
- queries: bfloat16 [16, 2048, 4096], P('grp', 'sp'), may hold values from -180 to 180
- keys: bfloat16 [16, 2048, 4096], P('grp', 'sp'), may hold values from -7 to 7
- values: bfloat16 [16, 2048, 4096], P('grp', 'sp'), may hold values from -6 to 6
- positions: int32 [16, 2048], P('grp'), may hold values from 0 to 2047, each once within a row
- anchor: int32 [1], replicated, may hold values from 0 to 1048575
Outputs:
- attended: bfloat16 [16, 2048, 4096], P('grp', 'sp')
The draws below stay inside these ranges and needn't reach their ends.
Inputs may be any that keep to these rules, and one draw needn't show every extreme that they name: Each group's row of positions holds every number of 0 to 2047 once.
All inputs are finite; a program needn't handle non-finite values.
Results may differ from the reference program's by a relative error of at most 0.0048.
Values may be sent and summed in bfloat16 or wider, within the bound.
A program may use at most 64 MiB of HBM per device.

```python
import math
import jax
import jax.numpy as jnp
from jax import lax

HD = 128
HEADS = 32
D = 4096
LEN = 2048
GROUPS = 16


def draw_keys(key, part):
    noise = jnp.clip(jax.random.normal(jax.random.fold_in(key, 12), (GROUPS, LEN, D), jnp.float32), -6.0, 6.0)
    result = noise
    return result.astype(jnp.bfloat16)


def draw_queries(key, part):
    noise = jnp.clip(jax.random.normal(jax.random.fold_in(key, 13), (GROUPS, LEN, D), jnp.float32), -6.0, 6.0)
    result = noise
    return result.astype(jnp.bfloat16)


def level_of(own_key, extent, pieces, least, largest):
    gain, own = 1.0, jax.random.fold_in(own_key, 6)
    for axis_at, parts in pieces:
        draws = jnp.exp(jax.random.uniform(jax.random.fold_in(own, axis_at), (parts,), jnp.float32, least / len(pieces), largest / len(pieces)))
        gain = gain * jnp.repeat(draws, extent[axis_at] // parts).reshape([-1 if axis == axis_at else 1 for axis in range(len(extent))])
    return gain


def centred(rng, shape, spread, bound, split=(), kind=jnp.bfloat16):
    loudness = level_of(rng, shape, split, -0.22, 0.18) if split else 1.0
    values = jax.random.normal(rng, shape, jnp.float32) * spread * loudness
    return jnp.minimum(jnp.maximum(values, -bound), bound).astype(kind)


def setup_inputs(seed: int = 0) -> dict:
    key_list = jax.random.split(jax.random.key(seed), 6)
    queries = draw_queries(jax.random.fold_in(key_list[5], 71), 0)
    keys = draw_keys(jax.random.fold_in(key_list[5], 71), 0)
    values = centred(key_list[2], (GROUPS, LEN, D), 1.0, 6.0, ((0, 16), (1, 32)))
    positions = jax.vmap(lambda own: jax.random.permutation(own, LEN))(jax.random.split(key_list[3], GROUPS)).reshape((GROUPS, LEN)).astype(jnp.int32)
    anchor = jax.random.randint(key_list[4], (1,), 0, GROUPS * 65536).astype(jnp.int32)
    return {"queries": queries, "keys": keys, "values": values, "positions": positions, "anchor": anchor}


NEG = -1e+30

def reference(queries, keys, values, positions, anchor):
    anchor_index = (anchor[0] % GROUPS).astype(jnp.int32)
    anchor_keys = keys[anchor_index]
    anchor_values = values[anchor_index]
    score_scale = 1.0 / math.sqrt(HD)

    def one_group(group_index):
        q_rows = queries[group_index]
        k_rows = keys[group_index]
        v_rows = values[group_index]
        order = positions[group_index]
        visible = order[None, :] <= order[:, None]
        skip_anchor = group_index == anchor_index

        def one_head(head_index):
            start = head_index * HD
            q_head = lax.dynamic_slice_in_dim(q_rows, start, HD, 1)
            k_head = lax.dynamic_slice_in_dim(k_rows, start, HD, 1)
            v_head = lax.dynamic_slice_in_dim(v_rows, start, HD, 1)
            ak_head = lax.dynamic_slice_in_dim(anchor_keys, start, HD, 1)
            av_head = lax.dynamic_slice_in_dim(anchor_values, start, HD, 1)
            local_scores = jnp.dot(q_head, k_head.T, preferred_element_type=jnp.float32) * score_scale
            far_scores = jnp.dot(q_head, ak_head.T, preferred_element_type=jnp.float32) * score_scale
            local_scores = jnp.where(visible, local_scores, NEG)
            far_scores = jnp.where(skip_anchor, NEG, far_scores)
            joined = jnp.concatenate([local_scores, far_scores], 1)
            top_score = lax.optimization_barrier(jnp.max(joined, axis=1, keepdims=True))
            expo = jnp.exp(joined - top_score)
            probs = (expo / lax.optimization_barrier(jnp.sum(expo, axis=1, keepdims=True))).astype(jnp.bfloat16)
            value_rows = jnp.concatenate([v_head, av_head], 0)
            return jnp.dot(probs, value_rows, preferred_element_type=jnp.float32).astype(jnp.bfloat16)
        per_head = lax.map(one_head, jnp.arange(HEADS, dtype=jnp.int32))
        return jnp.transpose(per_head, (1, 0, 2)).reshape(LEN, D)
    return lax.map(one_group, jnp.arange(GROUPS, dtype=jnp.int32))
```

```python
import functools
import math

import jax
import jax.numpy as jnp
from jax import lax
from jax.experimental import pallas as pl
from jax.experimental.pallas import tpu as pltpu
from jax.sharding import PartitionSpec as P

HD = 128
NEG = -1e30
NY = 4
NZ = 4
HALVES = 2
C = math.log2(math.e) / math.sqrt(HD)
MESH = pl.DeviceIdType.MESH
NT = (((1,), (1,)), ((), ()))


def scores_of(q, keys):
    return lax.dot_general(q, keys, NT, preferred_element_type=jnp.float32)


def weigh(s_scr, m, values, length):
    parts = [
        jnp.exp2(s_scr[:, j : j + 128] - m).astype(jnp.bfloat16)
        for j in range(0, length, 128)
    ]
    p = jnp.concatenate(parts, axis=1)
    wide = jnp.concatenate([values, jnp.ones_like(values)], axis=1)
    return jnp.dot(p, wide, preferred_element_type=jnp.float32)


def row_max(mx):
    return jnp.broadcast_to(jnp.max(mx, axis=1, keepdims=True), mx.shape)


def local_block(r0, bq, length, qh, kh, vh, posc, posr, s_scr, acc_loc, m_loc, l_loc):
    rows = pl.ds(r0, bq)
    s = scores_of(qh[rows, :], kh[...])
    mine = posc[rows, :]
    mx = jnp.full((bq, 128), NEG, jnp.float32)
    for j in range(0, length, 128):
        piece = jnp.where(mine >= posr[:, j : j + 128], s[:, j : j + 128] * C, NEG)
        s_scr[:, j : j + 128] = piece
        mx = jnp.maximum(mx, piece)
    m = row_max(mx)
    acc = weigh(s_scr, m, vh[...], length)
    acc_loc[rows, :] = acc[:, :HD]
    l_loc[rows, :] = acc[:, HD:]
    m_loc[rows, :] = m


def far_block(r0, bq, length, bias, qh, ak, av, s_scr, acc_loc, m_loc, l_loc, oh):
    rows = pl.ds(r0, bq)
    s = scores_of(qh[rows, :], ak[...])
    mx = jnp.full((bq, 128), NEG, jnp.float32)
    for j in range(0, length, 128):
        piece = s[:, j : j + 128] * C
        s_scr[:, j : j + 128] = piece
        mx = jnp.maximum(mx, piece)
    m_far = row_max(mx)
    acc = weigh(s_scr, m_far, av[...], length)
    m_far = m_far + bias
    m = jnp.maximum(m_loc[rows, :], m_far)
    w_loc = jnp.exp2(m_loc[rows, :] - m)
    w_far = jnp.exp2(m_far - m)
    top = acc_loc[rows, :] * w_loc + acc[:, :HD] * w_far
    bottom = l_loc[rows, :] * w_loc + acc[:, HD:] * w_far
    oh[rows, :] = (top / bottom).astype(jnp.bfloat16)


def kernel(
    shards, length, tokens, bq,
    anchor_ref, pos_ref, q_ref, k_ref, v_ref, out_ref,
    qh, kh, vh, ak, av, oh, posc, posr, s_scr, acc_loc, m_loc, l_loc,
    ybuf, abuf, bbuf,
    flat_send, flat_recv, y_send, y_recv, a_send, a_recv, b_send, b_recv, g_send, g_recv,
):
    grp = lax.axis_index("grp")
    me = lax.axis_index("sp")
    y = grp // NZ
    z = grp % NZ
    quarter = length // NY
    part = quarter // HALVES
    blocks = length // bq
    per_block = bq // tokens

    def pair_a(zz):
        return zz + 1 - 2 * (zz % 2)

    def pair_b(zz):
        return (zz + 3 + 2 * (zz % 2)) % NZ

    root = lax.rem(anchor_ref[0], NY * NZ)
    root_y = lax.div(root, NZ)
    root_z = lax.rem(root, NZ)
    pick_a = jnp.where(root_z == pair_a(z), 1, 0)
    pick_b = jnp.where((root_z == z) | (root_z == pair_a(z)), 0, 1)
    bias = jnp.where(root == grp, NEG, 0.0)

    barrier = pltpu.get_barrier_semaphore()

    def greet(d, carry):
        peer = lax.rem(me + d, shards)
        pl.semaphore_signal(barrier, inc=1, device_id=(grp, peer), device_id_type=MESH)
        return carry

    lax.fori_loop(1, shards, greet, 0)
    for d in range(1, NY):
        pl.semaphore_signal(
            barrier, inc=1, device_id=(((y + d) % NY) * NZ + z, me), device_id_type=MESH
        )
    for other in (pair_a(z), pair_b(z)):
        pl.semaphore_signal(
            barrier, inc=1, device_id=(y * NZ + other, me), device_id_type=MESH
        )

    posr[...] = pos_ref[...].astype(jnp.float32)
    for j in range(0, length, 128):
        square = jnp.broadcast_to(posr[:, j : j + 128], (128, 128))
        posc[j : j + 128, :] = square.T

    pl.semaphore_wait(barrier, shards - 1 + NY - 1 + 2)

    my_rows = pl.ds(pl.multiple_of(me * tokens, tokens), tokens)
    my_columns = pl.ds(pl.multiple_of(me * HD, HD), HD)

    def scatter(i, src, dst):
        pltpu.make_async_copy(
            src.at[0, :, my_columns], dst.at[my_rows, :], flat_recv.at[i]
        ).start()

        def body(n, carry):
            peer = lax.rem(me + lax.rem(n + shards // 4 - 1, shards - 1) + 1, shards)
            columns = pl.ds(pl.multiple_of(peer * HD, HD), HD)
            pltpu.make_async_remote_copy(
                src_ref=src.at[0, :, columns],
                dst_ref=dst.at[my_rows, :],
                send_sem=flat_send.at[i],
                recv_sem=flat_recv.at[i],
                device_id=(grp, peer),
                device_id_type=MESH,
            ).start()
            return carry

        lax.fori_loop(0, shards - 1, body, 0)

    def arrived(i, dst):
        pltpu.make_async_copy(dst, dst, flat_recv.at[i]).wait()

    def own_rows(j, h):
        return pl.ds(pl.multiple_of(j * quarter + h * part, part), part)

    def y_start(c, src):
        h = c % HALVES
        pltpu.make_async_copy(src.at[own_rows(y, h), :], ybuf[c].at[y], y_recv.at[c]).start()
        for d in range(1, NY):
            j = (y + d) % NY
            pltpu.make_async_remote_copy(
                src_ref=src.at[own_rows(j, h), :],
                dst_ref=ybuf[c].at[y],
                send_sem=y_send.at[c],
                recv_sem=y_recv.at[c],
                device_id=(j * NZ + z, me),
                device_id_type=MESH,
            ).start()

    def pair_copy(c, buf, send, recv, other):
        return pltpu.make_async_remote_copy(
            src_ref=buf[c].at[0],
            dst_ref=buf[c].at[1],
            send_sem=send.at[c],
            recv_sem=recv.at[c],
            device_id=(y * NZ + other, me),
            device_id_type=MESH,
        )

    def a_copy(c):
        return pair_copy(c, abuf, a_send, a_recv, pair_a(z))

    def b_copy(c):
        return pair_copy(c, bbuf, b_send, b_recv, pair_b(z))

    def a_start(c):
        pltpu.make_async_copy(ybuf[c], ybuf[c], y_recv.at[c]).wait()
        abuf[c][0] = ybuf[c][root_y]
        a_copy(c).start()

    def b_start(c):
        a_copy(c).wait_recv()
        bbuf[c][0] = abuf[c][pick_a]
        b_copy(c).start()

    def g_copies(c, dst):
        rows = own_rows(y, c % HALVES)
        return [
            pltpu.make_async_remote_copy(
                src_ref=dst.at[rows, :],
                dst_ref=dst.at[rows, :],
                send_sem=g_send.at[c],
                recv_sem=g_recv.at[c],
                device_id=(((y + d) % NY) * NZ + z, me),
                device_id_type=MESH,
            )
            for d in range(1, NY)
        ]

    def g_start(c, dst):
        b_copy(c).wait_recv()
        dst[own_rows(y, c % HALVES), :] = bbuf[c][pick_b]
        for copy in g_copies(c, dst):
            copy.start()

    def three(sem):
        view = ybuf[0].at[pl.ds(0, NY - 1)]
        pltpu.make_async_copy(view, view, sem).wait()

    parts = range(HALVES)
    first = [h for h in parts]
    second = [HALVES + h for h in parts]

    def block_row(i):
        turn = lax.rem(i + lax.div(me, per_block), blocks)
        return pl.multiple_of(turn * bq, bq)

    def local(low, high):
        def body(i, carry):
            local_block(
                block_row(i), bq, length, qh, kh, vh, posc, posr, s_scr, acc_loc, m_loc, l_loc
            )
            return carry

        lax.fori_loop(low, high, body, 0)

    scatter(0, k_ref, kh)
    scatter(1, v_ref, vh)
    arrived(0, kh)
    for c in first:
        y_start(c, kh)
    scatter(2, q_ref, qh)
    for c in first:
        a_start(c)
    arrived(1, vh)
    for c in second:
        y_start(c, vh)
    for c in first:
        b_start(c)
    for c in second:
        a_start(c)
    arrived(2, qh)
    step = max(1, blocks // 4)
    local(0, step)
    for c in first:
        g_start(c, ak)
    local(step, 2 * step)
    for c in second:
        b_start(c)
    local(2 * step, blocks)
    for c in second:
        g_start(c, av)
    for c in first + second:
        three(g_recv.at[c])

    def out_copies(i):
        turn = lax.rem(i + lax.div(me, per_block), blocks)
        for n in range(per_block):
            peer = turn * per_block + n
            rows = pl.ds(pl.multiple_of(peer * tokens, tokens), tokens)
            src = oh.at[rows, :]
            dst = out_ref.at[0, :, my_columns]

            @pl.when(peer == me)
            def _():
                pltpu.make_async_copy(src, dst, flat_recv.at[3]).start()

            @pl.when(peer != me)
            def _():
                pltpu.make_async_remote_copy(
                    src_ref=src,
                    dst_ref=dst,
                    send_sem=flat_send.at[3],
                    recv_sem=flat_recv.at[3],
                    device_id=(grp, peer),
                    device_id_type=MESH,
                ).start()

    def far(i, carry):
        far_block(
            block_row(i), bq, length, bias, qh, ak, av, s_scr, acc_loc, m_loc, l_loc, oh
        )
        out_copies(i)
        return carry

    lax.fori_loop(0, blocks, far, 0)

    most = pl.ds(0, (shards - 1) * tokens)
    for i, buf in enumerate((kh, vh, qh, oh)):
        pltpu.make_async_copy(buf.at[most, :], buf.at[most, :], flat_send.at[i]).wait()
    for c in first + second:
        three(y_send.at[c])
        a_copy(c).wait_send()
        b_copy(c).wait_send()
        three(g_send.at[c])
    pltpu.make_async_copy(out_ref, out_ref, flat_recv.at[3]).wait()


def solution(mesh):
    shards = mesh.shape["sp"]

    def on_device(queries, keys, values, positions, anchor):
        tokens = queries.shape[1]
        length = tokens * shards
        bq = max(tokens, min(256, length // 4))
        part = length // NY // HALVES
        chunks = 2 * HALVES
        bf16 = jnp.bfloat16
        head = pltpu.VMEM((length, HD), bf16)
        wide = pltpu.VMEM((length, HD), jnp.float32)
        dma = pltpu.SemaphoreType.DMA
        vmem = pl.BlockSpec(memory_space=pltpu.VMEM)
        return pl.pallas_call(
            functools.partial(kernel, shards, length, tokens, bq),
            out_shape=jax.ShapeDtypeStruct(queries.shape, bf16),
            in_specs=[pl.BlockSpec(memory_space=pltpu.SMEM), vmem, vmem, vmem, vmem],
            out_specs=vmem,
            scratch_shapes=[
                head, head, head, head, head, head,
                wide,
                pltpu.VMEM((1, length), jnp.float32),
                pltpu.VMEM((bq, length), jnp.float32),
                wide, wide, wide,
                [pltpu.VMEM((NY, part, HD), bf16)] * chunks,
                [pltpu.VMEM((2, part, HD), bf16)] * chunks,
                [pltpu.VMEM((2, part, HD), bf16)] * chunks,
                dma((4,)), dma((4,)),
                dma((chunks,)), dma((chunks,)),
                dma((chunks,)), dma((chunks,)),
                dma((chunks,)), dma((chunks,)),
                dma((chunks,)), dma((chunks,)),
            ],
            compiler_params=pltpu.CompilerParams(collective_id=0, has_side_effects=True),
            name="star_attention",
        )(anchor, positions, queries, keys, values)

    return jax.shard_map(
        on_device,
        mesh=mesh,
        in_specs=(
            P("grp", "sp", None),
            P("grp", "sp", None),
            P("grp", "sp", None),
            P("grp", None),
            P(),
        ),
        out_specs=P("grp", "sp", None),
        check_vma=False,
    )
```

```python
import functools
import math

import jax
import jax.numpy as jnp
from jax import lax
from jax.experimental import pallas as pl
from jax.experimental.pallas import tpu as pltpu
from jax.sharding import PartitionSpec as P

HD = 128
NEG = -1e30
NY = 4
NZ = 4
HALVES = 2
NL = 4
BQ = 512
C = math.log2(math.e) / math.sqrt(HD)
MESH = pl.DeviceIdType.MESH
NT = (((1,), (1,)), ((), ()))


def scores_of(q, keys):
    return lax.dot_general(q, keys, NT, preferred_element_type=jnp.float32)


def chances(s_scr, m, length):
    parts = [
        jnp.exp2(s_scr[:, j : j + 128] - m).astype(jnp.bfloat16)
        for j in range(0, length, 128)
    ]
    return jnp.concatenate(parts, axis=1)


def weigh(p, values):
    wide = jnp.concatenate([values, jnp.ones_like(values)], axis=1)
    return jnp.dot(p, wide, preferred_element_type=jnp.float32)


def row_max(mx):
    return jnp.broadcast_to(jnp.max(mx, axis=1, keepdims=True), mx.shape)


def local_block(r0, bq, length, qh, kh, vh, posc, posr, s_scr, acc_loc, m_loc, l_loc):
    rows = pl.ds(r0, bq)
    s = scores_of(qh[rows, :], kh[...])
    mine = posc[rows, :]
    mx = jnp.full((bq, 128), NEG, jnp.float32)
    for j in range(0, length, 128):
        piece = jnp.where(mine >= posr[:, j : j + 128], s[:, j : j + 128] * C, NEG)
        s_scr[:, j : j + 128] = piece
        mx = jnp.maximum(mx, piece)
    m = row_max(mx)
    acc = weigh(chances(s_scr, m, length), vh[...])
    acc_loc[rows, :] = acc[:, :HD]
    l_loc[rows, :] = acc[:, HD:]
    m_loc[rows, :] = m


def far_chances(r0, bq, length, qh, ak, s_scr, p_far, m_far):
    rows = pl.ds(r0, bq)
    s = scores_of(qh[rows, :], ak[...])
    mx = jnp.full((bq, 128), NEG, jnp.float32)
    for j in range(0, length, 128):
        piece = s[:, j : j + 128] * C
        s_scr[:, j : j + 128] = piece
        mx = jnp.maximum(mx, piece)
    m = row_max(mx)
    p_far[rows, :] = chances(s_scr, m, length)
    m_far[rows, :] = m


def far_block(r0, bq, bias, av, p_far, m_far, acc_loc, m_loc, l_loc, oh):
    rows = pl.ds(r0, bq)
    acc = weigh(p_far[rows, :], av[...])
    other = m_far[rows, :] + bias
    m = jnp.maximum(m_loc[rows, :], other)
    w_loc = jnp.exp2(m_loc[rows, :] - m)
    w_far = jnp.exp2(other - m)
    top = acc_loc[rows, :] * w_loc + acc[:, :HD] * w_far
    bottom = l_loc[rows, :] * w_loc + acc[:, HD:] * w_far
    oh[rows, :] = (top / bottom).astype(jnp.bfloat16)


def kernel(
    source, shards, length, tokens, bq,
    anchor_ref, pos_ref, q_ref, k_ref, v_ref, out_ref,
    qh, kh, vh, ak, av, oh, posc, posr, s_scr, p_far, acc_loc, m_loc, l_loc, m_far,
    ybuf,
    send, recv, q_recv, y_send, y_recv, z_send, z_recv, g_send, g_recv,
):
    grp = lax.axis_index("grp")
    me = lax.axis_index("sp")
    y = grp // NZ
    z = grp % NZ
    side = shards // NL
    zl = me // side
    spot = me % side
    step = (z + NZ - source) % NZ
    quarter = length // NY
    part = quarter // HALVES
    stretch = length // NL
    per_stretch = stretch // bq
    per_block = bq // tokens

    def head_of(lane):
        return lane + (z % 2) * (NL - 1 - 2 * lane)

    def turned(lane, d):
        if d == 0:
            return lane
        if d == 1:
            return lane + 1 - 2 * (lane % 2)
        if d == 2:
            return (lane + 2) % NL
        return NL - 1 - lane

    opposite = (NL - 1 - zl) * side + spot
    above = (y * NZ + (z + 1) % NZ, opposite)
    below = (y * NZ + (z + NZ - 1) % NZ, opposite)
    near_top = (zl // 2 + step) % 2

    root = lax.rem(anchor_ref[0], NY * NZ)
    root_y = lax.div(root, NZ)
    bias = jnp.where(root == grp, NEG, 0.0)

    barrier = pltpu.get_barrier_semaphore()

    def greet(d, carry):
        peer = lax.rem(me + d, shards)
        pl.semaphore_signal(barrier, inc=1, device_id=(grp, peer), device_id_type=MESH)
        return carry

    y_peers = [(((y + d) % NY) * NZ + z, me) for d in range(1, NY)]
    for peer in y_peers + [above, below]:
        pl.semaphore_signal(barrier, inc=1, device_id=peer, device_id_type=MESH)
    lax.fori_loop(1, shards, greet, 0)

    posr[...] = pos_ref[...].astype(jnp.float32)
    for j in range(0, length, 128):
        square = jnp.broadcast_to(posr[:, j : j + 128], (128, 128))
        posc[j : j + 128, :] = square.T

    pl.semaphore_wait(barrier, shards - 1 + NY - 1 + 2)

    my_rows = pl.ds(pl.multiple_of(me * tokens, tokens), tokens)
    my_head = head_of(zl) * side + spot
    my_columns = pl.ds(pl.multiple_of(my_head * HD, HD), HD)

    def remote(src, dst, send_sem, recv_sem, peer):
        return pltpu.make_async_remote_copy(
            src_ref=src,
            dst_ref=dst,
            send_sem=send_sem,
            recv_sem=recv_sem,
            device_id=peer,
            device_id_type=MESH,
        )

    def scatter(i, src, dst, recv_sem, order):
        for d in order:
            lane = turned(zl, d)

            def body(n, carry, lane=lane):
                place = lax.rem(spot + n, side)
                head = head_of(lane) * side + place
                columns = pl.ds(pl.multiple_of(head * HD, HD), HD)
                remote(
                    src.at[0, :, columns], dst.at[my_rows, :], send.at[i], recv_sem,
                    (grp, lane * side + place),
                ).start()
                return carry

            if d == 0:
                pltpu.make_async_copy(
                    src.at[0, :, my_columns], dst.at[my_rows, :], recv_sem
                ).start()
            lax.fori_loop(1 if d == 0 else 0, side, body, 0)

    def arrived(dst, sem):
        pltpu.make_async_copy(dst, dst, sem).wait()

    def own_rows(j, c):
        start = j * quarter + (c % HALVES) * part
        return pl.ds(pl.multiple_of(start, part), part)

    def y_start(c, src):
        pltpu.make_async_copy(src.at[own_rows(y, c), :], ybuf[c].at[y], y_recv.at[c]).start()
        for d in range(1, NY):
            j = (y + d) % NY
            remote(
                src.at[own_rows(j, c), :], ybuf[c].at[y], y_send.at[c], y_recv.at[c],
                (j * NZ + z, me),
            ).start()

    def z_copy(c, dst, peer):
        rows = dst.at[own_rows(y, c), :]
        return remote(rows, rows, z_send.at[c], z_recv.at[c], peer)

    def to_both(c, dst):
        arrived(ybuf[c], y_recv.at[c])
        dst[own_rows(y, c), :] = ybuf[c][root_y]
        z_copy(c, dst, above).start()
        z_copy(c, dst, below).start()

    passes_up = (step == 1) & (near_top == 0)
    passes_down = (step == NZ - 1) & (near_top == 1)

    def onward(c, dst):
        rows = dst.at[own_rows(y, c), :]
        arrived(rows, z_recv.at[c])

        @pl.when(passes_up)
        def _():
            z_copy(c, dst, above).start()

        @pl.when(passes_down)
        def _():
            z_copy(c, dst, below).start()

    def spread(c, dst):
        rows = dst.at[own_rows(y, c), :]
        for peer in y_peers:
            remote(rows, rows, g_send.at[c], g_recv.at[c], peer).start()

    def from_root(parts, dst):
        @pl.when(step == 0)
        def _():
            for c in parts:
                to_both(c, dst)
                spread(c, dst)

    def from_z(c, dst):
        @pl.when(step != 0)
        def _():
            onward(c, dst)
            spread(c, dst)

    def three(sem):
        arrived(ybuf[0].at[pl.ds(0, NY - 1)], sem)

    first = list(range(HALVES))
    second = [HALVES + h for h in first]

    scatter(0, k_ref, kh, recv.at[0], (2, 3, 1, 0))
    scatter(1, v_ref, vh, recv.at[1], (2, 3, 1, 0))
    scatter(2, q_ref, qh, q_recv.at[zl], (0, 1, 2, 3))

    arrived(kh, recv.at[0])

    @pl.when(step == 0)
    def _():
        for c in first:
            y_start(c, kh)

    from_root(first, ak)
    arrived(vh, recv.at[1])

    @pl.when(step == 0)
    def _():
        for c in second:
            y_start(c, vh)

    def lane_of(i):
        low = lax.rem(i, 2)
        flip = zl + low - 2 * low * (zl % 2)
        return lax.rem(flip + 2 * lax.div(i, 2), NL)

    def local(i, carry):
        lane = lane_of(i)

        @pl.when(i == 0)
        def _():
            from_z(first[0], ak)

        @pl.when(i == 1)
        def _():
            from_root(second, av)
            from_z(first[1], ak)

        @pl.when(i == 2)
        def _():
            from_z(second[0], av)

        @pl.when(i == 3)
        def _():
            from_z(second[1], av)

        base = pl.multiple_of(lane * stretch, stretch)
        arrived(qh.at[pl.ds(base, stretch), :], q_recv.at[lane])

        def body(n, inner):
            local_block(
                pl.multiple_of(base + n * bq, bq),
                bq, length, qh, kh, vh, posc, posr, s_scr, acc_loc, m_loc, l_loc,
            )
            return inner

        lax.fori_loop(0, per_stretch, body, 0)
        return carry

    lax.fori_loop(0, NL, local, 0)
    for c in first:
        three(g_recv.at[c])

    def block_start(i):
        lane = lane_of(NL - 1 - lax.div(i, per_stretch))
        turn = lax.rem(i + lax.div(spot, per_block), per_stretch)
        return pl.multiple_of(lane * stretch + turn * bq, bq)

    def far_first(i, carry):
        far_chances(block_start(i), bq, length, qh, ak, s_scr, p_far, m_far)
        return carry

    lax.fori_loop(0, NL * per_stretch, far_first, 0)
    for c in second:
        three(g_recv.at[c])

    def far_second(i, carry):
        r0 = block_start(i)
        far_block(r0, bq, bias, av, p_far, m_far, acc_loc, m_loc, l_loc, oh)
        for n in range(per_block):
            peer = lax.div(r0, tokens) + n
            rows = pl.ds(pl.multiple_of(peer * tokens, tokens), tokens)
            src = oh.at[rows, :]
            dst = out_ref.at[0, :, my_columns]

            @pl.when(peer == me)
            def _():
                pltpu.make_async_copy(src, dst, recv.at[2]).start()

            @pl.when(peer != me)
            def _():
                remote(src, dst, send.at[3], recv.at[2], (grp, peer)).start()

        return carry

    lax.fori_loop(0, NL * per_stretch, far_second, 0)

    most = pl.ds(0, (shards - 1) * tokens)
    for i, buf in enumerate((kh, vh, qh, oh)):
        arrived(buf.at[most, :], send.at[i])
    for c in first + second:
        three(g_send.at[c])

    @pl.when(step == 0)
    def _():
        for c in first + second:
            three(y_send.at[c])
            arrived(ybuf[c].at[pl.ds(0, 2)], z_send.at[c])

    @pl.when(passes_up | passes_down)
    def _():
        for c in first + second:
            arrived(ybuf[c].at[0], z_send.at[c])

    arrived(out_ref, recv.at[2])


def solution(mesh):
    shards = mesh.shape["sp"]

    def attend_from(source, anchor, positions, queries, keys, values):
        tokens = queries.shape[1]
        length = tokens * shards
        bq = max(tokens, min(BQ, length // NL))
        part = length // NY // HALVES
        chunks = 2 * HALVES
        bf16 = jnp.bfloat16
        head = pltpu.VMEM((length, HD), bf16)
        wide = pltpu.VMEM((length, HD), jnp.float32)
        dma = pltpu.SemaphoreType.DMA
        vmem = pl.BlockSpec(memory_space=pltpu.VMEM)
        return pl.pallas_call(
            functools.partial(kernel, source, shards, length, tokens, bq),
            out_shape=jax.ShapeDtypeStruct(queries.shape, bf16),
            in_specs=[pl.BlockSpec(memory_space=pltpu.SMEM), vmem, vmem, vmem, vmem],
            out_specs=vmem,
            scratch_shapes=[
                head, head, head, head, head, head,
                wide,
                pltpu.VMEM((1, length), jnp.float32),
                pltpu.VMEM((bq, length), jnp.float32),
                pltpu.VMEM((length, length), bf16),
                wide, wide, wide, wide,
                [pltpu.VMEM((NY, part, HD), bf16)] * chunks,
                dma((4,)), dma((3,)), dma((NL,)),
                dma((chunks,)), dma((chunks,)),
                dma((chunks,)), dma((chunks,)),
                dma((chunks,)), dma((chunks,)),
            ],
            compiler_params=pltpu.CompilerParams(
                collective_id=source, has_side_effects=True
            ),
            name=f"star_attention_{source}",
        )(anchor, positions, queries, keys, values)

    def on_device(queries, keys, values, positions, anchor):
        source = anchor[0] & (NZ - 1)
        branches = [functools.partial(attend_from, n) for n in range(NZ)]
        return lax.switch(source, branches, anchor, positions, queries, keys, values)

    return jax.shard_map(
        on_device,
        mesh=mesh,
        in_specs=(
            P("grp", "sp", None),
            P("grp", "sp", None),
            P("grp", "sp", None),
            P("grp", None),
            P(),
        ),
        out_specs=P("grp", "sp", None),
        check_vma=False,
    )
```

```python
import functools
import math

import jax
import jax.numpy as jnp
from jax import lax
from jax.experimental import pallas as pl
from jax.experimental.pallas import tpu as pltpu
from jax.sharding import PartitionSpec as P

HD = 128
NEG = -1e30
NY = 4
NZ = 4
NL = 4
BQ = 512
FIRST = (
    (0, 0), (0, 1), (1, 0), (1, 1), (0, 2), (0, 3),
    (1, 2), (1, 3), (2, 0), (2, 1),
)
LAST = ((2, 2), (2, 3))
C = math.log2(math.e) / math.sqrt(HD)
MESH = pl.DeviceIdType.MESH
NT = (((1,), (1,)), ((), ()))


def scores_of(q, keys):
    return lax.dot_general(q, keys, NT, preferred_element_type=jnp.float32)


def chances(s_scr, m, length):
    parts = [
        jnp.exp2(s_scr[:, j : j + 128] - m).astype(jnp.bfloat16)
        for j in range(0, length, 128)
    ]
    return jnp.concatenate(parts, axis=1)


def weigh(p, values):
    wide = jnp.concatenate([values, jnp.ones_like(values)], axis=1)
    return jnp.dot(p, wide, preferred_element_type=jnp.float32)


def row_max(mx):
    return jnp.broadcast_to(jnp.max(mx, axis=1, keepdims=True), mx.shape)


def local_block(r0, bq, length, qh, kh, vh, posc, posr, s_scr, acc_loc, m_loc, l_loc):
    rows = pl.ds(r0, bq)
    s = scores_of(qh[rows, :], kh[...])
    mine = posc[rows, :]
    mx = jnp.full((bq, 128), NEG, jnp.float32)
    for j in range(0, length, 128):
        piece = jnp.where(mine >= posr[:, j : j + 128], s[:, j : j + 128] * C, NEG)
        s_scr[:, j : j + 128] = piece
        mx = jnp.maximum(mx, piece)
    m = row_max(mx)
    acc = weigh(chances(s_scr, m, length), vh[...])
    acc_loc[rows, :] = acc[:, :HD]
    l_loc[rows, :] = acc[:, HD:]
    m_loc[rows, :] = m


def far_chances(r0, bq, length, qh, ak, s_scr, p_far, m_far):
    rows = pl.ds(r0, bq)
    s = scores_of(qh[rows, :], ak[...])
    mx = jnp.full((bq, 128), NEG, jnp.float32)
    for j in range(0, length, 128):
        piece = s[:, j : j + 128] * C
        s_scr[:, j : j + 128] = piece
        mx = jnp.maximum(mx, piece)
    m = row_max(mx)
    p_far[rows, :] = chances(s_scr, m, length)
    m_far[rows, :] = m


def far_block(r0, bq, bias, av, p_far, m_far, acc_loc, m_loc, l_loc, oh):
    rows = pl.ds(r0, bq)
    acc = weigh(p_far[rows, :], av[...])
    other = m_far[rows, :] + bias
    m = jnp.maximum(m_loc[rows, :], other)
    w_loc = jnp.exp2(m_loc[rows, :] - m)
    w_far = jnp.exp2(other - m)
    top = acc_loc[rows, :] * w_loc + acc[:, :HD] * w_far
    bottom = l_loc[rows, :] * w_loc + acc[:, HD:] * w_far
    oh[rows, :] = (top / bottom).astype(jnp.bfloat16)


def kernel(
    source, shards, length, tokens, bq,
    anchor_ref, pos_ref, q_ref, k_ref, v_ref, out_ref,
    qh, kh, vh, ak, av, oh, posc, posr, s_scr, p_far, acc_loc, m_loc, l_loc, m_far,
    ybuf,
    send, recv, lane_recv, y_send, y_recv, z_send, z_recv, g_send, g_recv,
):
    grp = lax.axis_index("grp")
    me = lax.axis_index("sp")
    y = grp // NZ
    z = grp % NZ
    side = shards // NL
    zl = me // side
    spot = me % side
    step = (z + NZ - source) % NZ
    stretch = length // NL
    part = stretch // NY
    per_stretch = stretch // bq
    per_block = bq // tokens

    def head_of(lane):
        return lane + (z % 2) * (NL - 1 - 2 * lane)

    def turned(lane, d):
        if d == 0:
            return lane
        if d == 1:
            return lane + 1 - 2 * (lane % 2)
        if d == 2:
            return (lane + 2) % NL
        return NL - 1 - lane

    opposite = (NL - 1 - zl) * side + spot
    above = (y * NZ + (z + 1) % NZ, opposite)
    below = (y * NZ + (z + NZ - 1) % NZ, opposite)
    near_top = (zl // 2 + step) % 2

    root = lax.rem(anchor_ref[0], NY * NZ)
    root_y = lax.div(root, NZ)
    bias = jnp.where(root == grp, NEG, 0.0)

    barrier = pltpu.get_barrier_semaphore()

    def greet(d, carry):
        peer = lax.rem(me + d, shards)
        pl.semaphore_signal(barrier, inc=1, device_id=(grp, peer), device_id_type=MESH)
        return carry

    y_peers = [(((y + d) % NY) * NZ + z, me) for d in range(1, NY)]
    for peer in y_peers + [above, below]:
        pl.semaphore_signal(barrier, inc=1, device_id=peer, device_id_type=MESH)
    lax.fori_loop(1, shards, greet, 0)

    posr[...] = pos_ref[...].astype(jnp.float32)
    for j in range(0, length, 128):
        square = jnp.broadcast_to(posr[:, j : j + 128], (128, 128))
        posc[j : j + 128, :] = square.T

    pl.semaphore_wait(barrier, shards - 1 + NY - 1 + 2)

    my_rows = pl.ds(pl.multiple_of(me * tokens, tokens), tokens)
    my_head = head_of(zl) * side + spot
    my_columns = pl.ds(pl.multiple_of(my_head * HD, HD), HD)

    def remote(src, dst, send_sem, recv_sem, peer):
        return pltpu.make_async_remote_copy(
            src_ref=src,
            dst_ref=dst,
            send_sem=send_sem,
            recv_sem=recv_sem,
            device_id=peer,
            device_id_type=MESH,
        )

    def scatter(i, src, dst, recv_sem, order):
        for d in order:
            lane = turned(zl, d)

            def body(n, carry, lane=lane):
                place = lax.rem(spot + n, side)
                head = head_of(lane) * side + place
                columns = pl.ds(pl.multiple_of(head * HD, HD), HD)
                remote(
                    src.at[0, :, columns], dst.at[my_rows, :], send.at[i], recv_sem,
                    (grp, lane * side + place),
                ).start()
                return carry

            if d == 0:
                pltpu.make_async_copy(
                    src.at[0, :, my_columns], dst.at[my_rows, :], recv_sem
                ).start()
            lax.fori_loop(1 if d == 0 else 0, side, body, 0)

    def arrived(dst, sem):
        pltpu.make_async_copy(dst, dst, sem).wait()

    root_zl = zl + (step % 2) * (NL - 1 - 2 * zl)

    def own_rows(j, c):
        start = turned(root_zl, c % NL) * stretch + j * part
        return pl.ds(pl.multiple_of(start, part), part)

    def y_start(c, src):
        pltpu.make_async_copy(src.at[own_rows(y, c), :], ybuf[c].at[y], y_recv.at[c]).start()
        for d in range(1, NY):
            j = (y + d) % NY
            remote(
                src.at[own_rows(j, c), :], ybuf[c].at[y], y_send.at[c], y_recv.at[c],
                (j * NZ + z, me),
            ).start()

    def z_copy(c, dst, peer):
        rows = dst.at[own_rows(y, c), :]
        return remote(rows, rows, z_send.at[c], z_recv.at[c], peer)

    def to_both(c, dst):
        arrived(ybuf[c], y_recv.at[c])
        dst[own_rows(y, c), :] = ybuf[c][root_y]
        z_copy(c, dst, above).start()
        z_copy(c, dst, below).start()

    passes_up = (step == 1) & (near_top == 0)
    passes_down = (step == NZ - 1) & (near_top == 1)

    def onward(c, dst):
        rows = dst.at[own_rows(y, c), :]
        arrived(rows, z_recv.at[c])

        @pl.when(passes_up)
        def _():
            z_copy(c, dst, above).start()

        @pl.when(passes_down)
        def _():
            z_copy(c, dst, below).start()

    def spread(c, dst):
        rows = dst.at[own_rows(y, c), :]
        for peer in y_peers:
            remote(rows, rows, g_send.at[c], g_recv.at[c], peer).start()

    def three(sem):
        arrived(ybuf[0].at[pl.ds(0, NY - 1)], sem)

    keys = list(range(NL))
    values = [NL + d for d in keys]

    def scatter_all(plan):
        tensors = ((k_ref, kh), (v_ref, vh), (q_ref, qh))
        for i, d in plan:
            src, dst = tensors[i]
            scatter(i, src, dst, lane_recv.at[i, zl], (d,))

    def stretch_in(c):
        lane = turned(zl, c % NL)
        buf = (kh, vh)[c // NL]
        rows = pl.ds(pl.multiple_of(lane * stretch, stretch), stretch)
        arrived(buf.at[rows, :], lane_recv.at[c // NL, lane])

        @pl.when(step == 0)
        def _():
            y_start(c, buf)

    def from_root(*parts):
        @pl.when(step == 0)
        def _():
            for c in parts:
                dst = (ak, av)[c // NL]
                to_both(c, dst)
                spread(c, dst)

    def from_z(*parts):
        @pl.when(step != 0)
        def _():
            for c in parts:
                dst = (ak, av)[c // NL]
                onward(c, dst)
                spread(c, dst)

    scatter_all(FIRST)
    k0, k1, k2, k3 = keys
    v0, v1, v2, v3 = values
    stretch_in(k0)
    stretch_in(k1)
    stretch_in(v0)
    from_root(k0)
    stretch_in(v1)
    from_root(k1, v0, v1)
    from_z(k0, k1)
    stretch_in(k2)
    stretch_in(k3)

    @pl.when(step != 0)
    def _():
        scatter_all(LAST)

    from_root(k2, k3)
    from_z(v0, v1, k2, k3)
    stretch_in(v2)
    stretch_in(v3)
    from_root(v2, v3)

    @pl.when(step == 0)
    def _():
        scatter_all(LAST)

    def lane_of(i):
        low = lax.rem(i, 2)
        flip = zl + low - 2 * low * (zl % 2)
        return lax.rem(flip + 2 * lax.div(i, 2), NL)

    def middle(n, carry):
        is_local = (n < 3) | (n == 6)
        i = jnp.where(n < 3, n, jnp.where(n < 6, n - 3, 3))
        lane = lane_of(i)
        base = pl.multiple_of(lane * stretch, stretch)

        @pl.when(n == 2)
        def _():
            from_z(v2)

        @pl.when(n == 3)
        def _():
            from_z(v3)
            for c in keys:
                three(g_recv.at[c])

        @pl.when(is_local)
        def _():
            arrived(qh.at[pl.ds(base, stretch), :], lane_recv.at[2, lane])

            def body(m, inner):
                local_block(
                    pl.multiple_of(base + m * bq, bq),
                    bq, length, qh, kh, vh, posc, posr, s_scr, acc_loc, m_loc, l_loc,
                )
                return inner

            lax.fori_loop(0, per_stretch, body, 0)

        @pl.when(jnp.logical_not(is_local))
        def _():
            def body(m, inner):
                far_chances(
                    pl.multiple_of(base + m * bq, bq), bq, length, qh, ak, s_scr, p_far, m_far
                )
                return inner

            lax.fori_loop(0, per_stretch, body, 0)

        return carry

    lax.fori_loop(0, 2 * NL, middle, 0)
    for c in values:
        three(g_recv.at[c])

    def block_start(i):
        lane = lane_of(NL - 1 - lax.div(i, per_stretch))
        turn = lax.rem(i + lax.div(spot, per_block), per_stretch)
        return pl.multiple_of(lane * stretch + turn * bq, bq)

    def far_second(i, carry):
        r0 = block_start(i)
        far_block(r0, bq, bias, av, p_far, m_far, acc_loc, m_loc, l_loc, oh)
        for n in range(per_block):
            peer = lax.div(r0, tokens) + n
            rows = pl.ds(pl.multiple_of(peer * tokens, tokens), tokens)
            src = oh.at[rows, :]
            dst = out_ref.at[0, :, my_columns]

            @pl.when(peer == me)
            def _():
                pltpu.make_async_copy(src, dst, recv.at[2]).start()

            @pl.when(peer != me)
            def _():
                remote(src, dst, send.at[3], recv.at[2], (grp, peer)).start()

        return carry

    lax.fori_loop(0, NL * per_stretch, far_second, 0)

    most = pl.ds(0, (shards - 1) * tokens)
    for i, buf in enumerate((kh, vh, qh, oh)):
        arrived(buf.at[most, :], send.at[i])
    for c in keys + values:
        three(g_send.at[c])

    @pl.when(step == 0)
    def _():
        for c in keys + values:
            three(y_send.at[c])
            arrived(ybuf[c].at[pl.ds(0, 2)], z_send.at[c])

    @pl.when(passes_up | passes_down)
    def _():
        for c in keys + values:
            arrived(ybuf[c].at[0], z_send.at[c])

    arrived(out_ref, recv.at[2])


def solution(mesh):
    shards = mesh.shape["sp"]

    def attend_from(source, anchor, positions, queries, keys, values):
        tokens = queries.shape[1]
        length = tokens * shards
        bq = max(tokens, min(BQ, length // NL))
        part = length // NL // NY
        chunks = 2 * NL
        bf16 = jnp.bfloat16
        head = pltpu.VMEM((length, HD), bf16)
        wide = pltpu.VMEM((length, HD), jnp.float32)
        dma = pltpu.SemaphoreType.DMA
        vmem = pl.BlockSpec(memory_space=pltpu.VMEM)
        return pl.pallas_call(
            functools.partial(kernel, source, shards, length, tokens, bq),
            out_shape=jax.ShapeDtypeStruct(queries.shape, bf16),
            in_specs=[pl.BlockSpec(memory_space=pltpu.SMEM), vmem, vmem, vmem, vmem],
            out_specs=vmem,
            scratch_shapes=[
                head, head, head, head, head, head,
                wide,
                pltpu.VMEM((1, length), jnp.float32),
                pltpu.VMEM((bq, length), jnp.float32),
                pltpu.VMEM((length, length), bf16),
                wide, wide, wide, wide,
                [pltpu.VMEM((NY, part, HD), bf16)] * chunks,
                dma((4,)), dma((3,)), dma((3, NL)),
                dma((chunks,)), dma((chunks,)),
                dma((chunks,)), dma((chunks,)),
                dma((chunks,)), dma((chunks,)),
            ],
            compiler_params=pltpu.CompilerParams(
                collective_id=source, has_side_effects=True
            ),
            name=f"star_attention_{source}",
        )(anchor, positions, queries, keys, values)

    def on_device(queries, keys, values, positions, anchor):
        source = anchor[0] & (NZ - 1)
        branches = [functools.partial(attend_from, n) for n in range(NZ)]
        return lax.switch(source, branches, anchor, positions, queries, keys, values)

    return jax.shard_map(
        on_device,
        mesh=mesh,
        in_specs=(
            P("grp", "sp", None),
            P("grp", "sp", None),
            P("grp", "sp", None),
            P("grp", None),
            P(),
        ),
        out_specs=P("grp", "sp", None),
        check_vma=False,
    )
```
